32 devices in a mesh: grp: 2 (over y), lon: 4 (over x, core), lat: 4 (over z).
Axes of the slice: x: 2, y: 2, z: 4, core: 2. Of those that a mesh axis runs over, the one named last changes fastest.
Arguments:
- tracers: float32 [4, 64, 128, 128], P('grp', 'lat', 'lon'), parts along dimension 0, may hold values from -6 to 6
- adjoint_in: float32 [4, 64, 128, 128], P('grp', 'lat', 'lon'), parts along dimension 0, may hold values from -6 to 6
- shifts: int32 [2, 64], replicated, may hold values from 0 to 127, as said below
- fractions: float32 [2, 64], replicated, may hold values from 0.05 to 0.95
- meridional: float32 [2, 64, 128], P(None, None, 'lon'), may hold values from -0.9 to 0.9
Outputs:
- advected: float32 [4, 64, 128, 128], P('grp', 'lat', 'lon'), parts along dimension 0
- adjoint_out: float32 [4, 64, 128, 128], P('grp', 'lat', 'lon'), parts along dimension 0
The draws below stay inside these ranges and needn't reach their ends.
There are 2 independent parts, one for each index of `grp`. The reference program is written for one: setup_inputs(seed, part) draws one part's arguments, and reference() takes and returns one part's arrays. A program takes and returns all parts, laid end to end along the dimension named above; an argument that names none is the same for every part. Nothing has to cross between parts.
Inputs may be any that keep to these rules, and one draw needn't show every extreme that they name: At row j, shifts lie below 1 + (127) d^2 / 63^2 with d = |2j - 63|.
All inputs are finite; a program needn't handle non-finite values.
Results may differ from the reference program's by a relative error of at most 0.0003.
Values sent between devices are 32-bit elements; how exact they have to be, the bound alone decides.
No kernel may reach another device: no remote copies, remote signals or barrier semaphores. Data moves between devices by JAX's collectives and lax.ppermute only.
A program may use at most 128 MiB of HBM per device.

```python
import jax
import jax.numpy as jnp
from jax import lax

C = 128
LEV = 2
NX = 128
NY = 64


def draw_shifts(key, part):
    row_ids = jnp.arange(NY, dtype=jnp.int32)
    distance = jnp.abs(2 * row_ids + 1 - NY)
    ceiling = 1 + (NX - 1) * distance * distance // ((NY - 1) * (NY - 1))
    drawn = jax.random.randint(key, (LEV, NY), 0, ceiling[None, :], dtype=jnp.int32)
    drawn = drawn.at[0, 0].set(NX - 1)
    drawn = drawn.at[0, NY // 2].set(0)
    return drawn


def steps_of(own_key, extent, shards, least, largest):
    level = 1.0
    for axis_at, shards_of in shards:
        draws = jax.random.uniform(jax.random.fold_in(jax.random.fold_in(own_key, 6), axis_at), (shards_of,), jnp.float32, least / len(shards), largest / len(shards))
        level = level * jnp.repeat(jnp.exp(draws), extent[axis_at] // shards_of).reshape((-1,) + (1,) * (len(extent) - 1 - axis_at))
    return level


def noise(stream_key, dims, scale, reach, pieces=(), kind=jnp.bfloat16):
    values = scale * jax.random.normal(stream_key, dims, jnp.float32)
    if pieces:
        values = values * steps_of(stream_key, dims, pieces, -0.22, 0.18)
    return jnp.clip(values, -reach, reach).astype(kind)


def setup_inputs(seed: int = 0, part: int = 0) -> dict:
    seeds = jax.random.split(jax.random.key(seed), 6)
    part_keys = jax.random.split(jax.random.fold_in(seeds[5], part), 6)
    return {
        "tracers": noise(part_keys[0], (LEV, NY, NX, C), 1.0, 6.0, ((1, 4), (2, 4)), jnp.float32),
        "adjoint_in": noise(part_keys[1], (LEV, NY, NX, C), 1.0, 6.0, ((1, 4), (2, 4)), jnp.float32),
        "shifts": draw_shifts(jax.random.fold_in(seeds[5], 71), part),
        "fractions": jnp.clip(jax.random.uniform(seeds[3], (LEV, NY), jnp.float32, 0.05, 0.95), 0.05, 0.95),
        "meridional": jnp.clip(jax.random.uniform(seeds[4], (LEV, NY, NX), jnp.float32, -0.9, 0.9) * steps_of(seeds[4], (LEV, NY, NX), ((2, 4),), -0.4, 0.0), -0.9, 0.9),
    }


def take_slice(values_in, start_at, stop_at, dimension):
    return lax.slice_in_dim(values_in, start_at, stop_at, axis=dimension)

def edge_values(values_in, amount, dimension):
    inner_sum = take_slice(values_in, 1, amount + 1, dimension) + take_slice(values_in, 2, amount + 2, dimension)
    outer_sum = take_slice(values_in, 0, amount, dimension) + take_slice(values_in, 3, amount + 3, dimension)
    return (7.0 * inner_sum - outer_sum) / 12.0

def cell_profile(values_in, dimension):
    interior = values_in.shape[dimension] - 6
    edge_row = edge_values(values_in, interior + 3, dimension)
    left_edge = take_slice(edge_row, 0, interior + 2, dimension)
    right_edge = take_slice(edge_row, 1, interior + 3, dimension)
    centres = take_slice(values_in, 2, interior + 4, dimension)
    curvature = 6.0 * centres - 3.0 * (left_edge + right_edge)
    return (interior, left_edge, right_edge, right_edge - left_edge, curvature)

def zonal_step(values_in, courant, dimension):
    interior, left_edge, right_edge, difference, curvature = cell_profile(values_in, dimension)
    transport = courant * (right_edge - 0.5 * courant * (difference - (1.0 - courant * (2.0 / 3.0)) * curvature))
    return take_slice(values_in, 3, interior + 3, dimension) - take_slice(transport, 1, interior + 1, dimension) + take_slice(transport, 0, interior, dimension)

def meridional_step(values_in, face_courant, dimension):
    interior, left_edge, right_edge, difference, curvature = cell_profile(values_in, dimension)

    def below_part(source):
        return take_slice(source, 0, interior + 1, dimension)

    def above_part(source):
        return take_slice(source, 1, interior + 2, dimension)
    northward = face_courant * (below_part(right_edge) - 0.5 * face_courant * (below_part(difference) - (1.0 - face_courant * (2.0 / 3.0)) * below_part(curvature)))
    southward = face_courant * (above_part(left_edge) - 0.5 * face_courant * above_part(difference) - above_part(curvature) * (0.5 * face_courant + face_courant * face_courant / 3.0))
    transport = jnp.where(face_courant > 0.0, northward, southward)
    return take_slice(values_in, 3, interior + 3, dimension) - take_slice(transport, 1, interior + 1, dimension) + take_slice(transport, 0, interior, dimension)

def advect_level(values_in, shift_row, fraction_row, face_level):
    width_cells = values_in.shape[1]
    positions = jnp.mod(jnp.arange(width_cells, dtype=jnp.int32)[None, :] - shift_row[:, None].astype(jnp.int32), width_cells).astype(jnp.int32)
    shifted = jnp.take_along_axis(values_in, positions[:, :, None], axis=1)
    wrapped = jnp.concatenate([shifted[:, -3:], shifted, shifted[:, :3]], axis=1)
    zonal = zonal_step(wrapped, fraction_row[:, None, None], 1)
    padded = jnp.pad(zonal, ((3, 3), (0, 0), (0, 0)))
    return meridional_step(padded, face_level[:, :, None], 0)

def reference(tracers, adjoint_in, shifts, fractions, meridional):
    forward_levels = []
    backward_levels = []
    for level_index in range(LEV):
        zero_row = jnp.zeros((1, NX), meridional.dtype)
        face_level = jnp.concatenate([zero_row, meridional[level_index, 1:], zero_row], axis=0)

        def one_level(values_in):
            return advect_level(values_in, shifts[level_index], fractions[level_index], face_level)
        result, pullback = jax.vjp(one_level, tracers[level_index])
        forward_levels.append(result)
        backward_levels.append(pullback(adjoint_in[level_index])[0])
    return (jnp.stack(forward_levels), jnp.stack(backward_levels))
```

```python
import jax
import jax.numpy as jnp
from jax import lax
from jax.experimental import pallas as pl
from jax.experimental.pallas import tpu as pltpu
from jax.sharding import PartitionSpec as P


HALO = 3
TAPS = 6
VMEM = pl.BlockSpec(memory_space=pltpu.VMEM)
SMEM = pl.BlockSpec(memory_space=pltpu.SMEM)


def swap_lon(value, bit):
    count = lax.axis_size("lon")
    return lax.ppermute(value, "lon", [(i, i ^ bit) for i in range(count)])


def swap_lat(value, odd):
    count = lax.axis_size("lat")
    pairs = []
    for i in range(count):
        j = ((i + 1) ^ 1) - 1 if odd else i ^ 1
        pairs.append((i, j if 0 <= j < count else i))
    return lax.ppermute(value, "lat", pairs)


def gather_lon(own):
    blocks = {0: own}
    bit = lax.axis_size("lon") // 2
    while bit:
        blocks.update({k ^ bit: swap_lon(b, bit) for k, b in list(blocks.items())})
        bit //= 2
    return [blocks[k] for k in range(len(blocks))]


def zonal_taps(courant):
    a = courant * courant * (3.0 - 2.0 * courant)
    b = courant * (1.0 - courant) * (1.0 - courant)
    g = -courant * courant * (1.0 - courant)
    zero = jnp.zeros_like(courant)
    f = [zero, -g, 7.0 * g - b, 12.0 * a + 7.0 * (b + g), 7.0 * b - g, -b, zero]
    taps = [(f[t + 1] - f[t]) / 12.0 for t in range(TAPS)]
    taps[HALO] = taps[HALO] + 1.0
    return taps


def sweep_body(starts, taps, place, blocks, ring):
    count = len(blocks)
    levels, rows, cells, _ = blocks[0].shape
    total = count * cells
    me = place[0]

    def fill(row, carry):
        level, j = row // rows, row % rows
        for k, block in enumerate(blocks):
            slot = pl.multiple_of((me ^ k) * cells, cells)
            ring[row, pl.ds(slot, cells), :] = block[level, j]
        ring[row, pl.ds(total, cells + 8), :] = ring[row, pl.ds(0, cells + 8), :]
        return carry

    lax.fori_loop(0, levels * rows, fill, 0, unroll=4)

    def one(row):
        p = starts[row]
        acc = taps[row * TAPS] * ring[row, pl.ds(p, cells), :]
        for t in range(1, TAPS):
            acc = acc + taps[row * TAPS + t] * ring[row, pl.ds(p + t, cells), :]
        return acc

    return one


def zonal_call(blocks, starts, taps, place, edges):
    levels, rows, cells, tracers = blocks[0].shape
    count = len(blocks)

    def kernel(starts_ref, taps_ref, place_ref, *refs):
        ins, outs, ring = refs[:count], refs[count:-1], refs[-1]
        one = sweep_body(starts_ref, taps_ref, place_ref, ins, ring)

        def go(row, carry):
            outs[0][row // rows, row % rows] = one(row)
            return carry

        lax.fori_loop(0, levels * rows, go, 0, unroll=4)
        if edges:
            for out, at in zip(outs[1:], (place_ref[1], place_ref[2])):
                for level in range(levels):
                    for r in range(HALO):
                        out[level, r] = outs[0][level, at + r]

    whole = jax.ShapeDtypeStruct(blocks[0].shape, jnp.float32)
    edge = jax.ShapeDtypeStruct((levels, HALO, cells, tracers), jnp.float32)
    shapes = (whole, edge, edge) if edges else (whole,)
    return pl.pallas_call(
        kernel,
        out_shape=shapes,
        in_specs=[SMEM] * 3 + [VMEM] * count,
        out_specs=tuple([VMEM] * len(shapes)),
        scratch_shapes=[pltpu.VMEM((levels * rows, count * cells + cells + 8, tracers), jnp.float32)],
        name="zonal_forward" if edges else "zonal_adjoint",
    )(starts, taps, place, *blocks)


def face_terms(v):
    s = jnp.abs(v)
    r = 1.0 - s
    return v * s * (3.0 - 2.0 * s), v * r * r, -v * s * r, v > 0.0


def padded_rows(own, first, second, place, level, cut, masked):
    rows = own.shape[1]
    even = place[3] == 1

    def halo(r, low):
        a, b = first[level, r, cut], second[level, r, cut]
        value = jnp.where(even, b, a) if low else jnp.where(even, a, b)
        if masked:
            keep = place[4] if low else place[5]
            value = jnp.where(keep == 1, value, 0.0)
        return value

    low = [halo(r, True) for r in range(HALO)]
    high = [halo(r, False) for r in range(HALO)]
    return low + [own[level, r, cut] for r in range(rows)] + high


def meridional_call(own, first, second, faces, place, adjoint):
    levels, rows, cells, tracers = own.shape
    step = 8

    def forward(z, v, level, cut, out):
        e = [
            (7.0 * (z[k + 1] + z[k + 2]) - (z[k] + z[k + 3])) * (1.0 / 12.0)
            for k in range(rows + 3)
        ]
        flux = []
        for k in range(rows + 1):
            a, b, g, pos = face_terms(v(k + 2))
            up = jnp.where(pos, z[k + 2], z[k + 3])
            far = jnp.where(pos, e[k], e[k + 2])
            flux.append(a * up + b * e[k + 1] + g * far)
        for m in range(rows):
            out[level, m, cut] = z[m + 3] - flux[m + 1] + flux[m]

    def backward(y, v, level, cut, out):
        ap, an, bg, gp, gn = [], [], [], [], []
        for q in range(rows + 5):
            a, b, g, pos = face_terms(v(q))
            d = y[q + 1] - y[q]
            ad, gd = a * d, g * d
            ap.append(jnp.where(pos, ad, 0.0))
            an.append(jnp.where(pos, 0.0, ad))
            bg.append(b * d)
            gp.append(jnp.where(pos, gd, 0.0))
            gn.append(jnp.where(pos, 0.0, gd))
        e = [None] + [bg[q] + gp[q + 1] + gn[q - 1] for q in range(1, rows + 4)]
        for m in range(rows):
            spread = (7.0 * (e[m + 2] + e[m + 3]) - (e[m + 4] + e[m + 1])) * (1.0 / 12.0)
            out[level, m, cut] = y[m + 3] + ap[m + 3] + an[m + 2] + spread

    def kernel(place_ref, own_ref, first_ref, second_ref, faces_ref, out_ref):
        def go(chunk, carry):
            level, part = chunk // (cells // step), chunk % (cells // step)
            cut = pl.ds(pl.multiple_of(part * step, step), step)

            def v(q):
                return jnp.broadcast_to(faces_ref[level, cut, q : q + 1], (step, tracers))

            rows_in = padded_rows(own_ref, first_ref, second_ref, place_ref, level, cut, not adjoint)
            (backward if adjoint else forward)(rows_in, v, level, cut, out_ref)
            return carry

        lax.fori_loop(0, levels * (cells // step), go, 0)

    return pl.pallas_call(
        kernel,
        out_shape=jax.ShapeDtypeStruct(own.shape, jnp.float32),
        in_specs=[SMEM] + [VMEM] * 4,
        out_specs=VMEM,
        name="meridional_adjoint" if adjoint else "meridional_forward",
    )(place, own, first, second, faces)


def local(tracers, adjoint_in, shifts, fractions, meridional):
    levels, rows, cells, _ = tracers.shape
    lon, lat = lax.axis_index("lon"), lax.axis_index("lat")
    lats = lax.axis_size("lat")
    total = cells * lax.axis_size("lon")
    first_row = lat * rows
    my_shifts = lax.dynamic_slice_in_dim(shifts, first_row, rows, 1).reshape(-1)
    my_fractions = lax.dynamic_slice_in_dim(fractions, first_row, rows, 1)
    taps = zonal_taps(my_fractions)
    forward_taps = jnp.stack(taps, -1).reshape(-1)
    adjoint_taps = jnp.stack(taps[::-1], -1).reshape(-1)
    forward_starts = jnp.mod(lon * cells - my_shifts - HALO, total)
    adjoint_starts = jnp.mod(lon * cells + my_shifts - (TAPS - 1 - HALO), total)
    even = lat % 2 == 0
    top = rows - HALO
    place = jnp.stack(
        [
            lon,
            jnp.where(even, top, 0),
            jnp.where(even, 0, top),
            even.astype(jnp.int32),
            (lat > 0).astype(jnp.int32),
            (lat < lats - 1).astype(jnp.int32),
        ]
    ).astype(jnp.int32)
    row_ids = jnp.arange(shifts.shape[1], dtype=jnp.int32)[None, :, None]
    face_values = jnp.where(row_ids > 0, meridional, 0.0)
    padded_faces = jnp.pad(face_values, ((0, 0), (3, 4), (0, 0)))
    faces = lax.dynamic_slice_in_dim(padded_faces, first_row + 1, rows + 5, 1)
    faces = jnp.swapaxes(faces, 1, 2)

    forward_blocks = gather_lon(tracers)

    give_first = lax.dynamic_slice_in_dim(adjoint_in, place[1], HALO, 1)
    give_second = lax.dynamic_slice_in_dim(adjoint_in, place[2], HALO, 1)
    pulled = meridional_call(
        adjoint_in, swap_lat(give_first, False), swap_lat(give_second, True), faces, place, True
    )
    adjoint_blocks = gather_lon(pulled)

    zonal, edge_first, edge_second = zonal_call(forward_blocks, forward_starts, forward_taps, place, True)
    advected = meridional_call(
        zonal, swap_lat(edge_first, False), swap_lat(edge_second, True), faces, place, False
    )
    (adjoint_out,) = zonal_call(adjoint_blocks, adjoint_starts, adjoint_taps, place, False)
    return advected, adjoint_out


def solution(mesh):
    field = P("grp", "lat", "lon", None)
    return jax.shard_map(
        local,
        mesh=mesh,
        in_specs=(field, field, P(), P(), P(None, None, "lon")),
        out_specs=(field, field),
        check_vma=False,
    )
```
